32 devices in a mesh: seq: 8 (over z, y), ch: 4 (over x, core).
Axes of the slice: x: 2, y: 2, z: 4, core: 2. Of those that a mesh axis runs over, the one named last changes fastest.
Arguments:
- queries: float32 [1024, 1024], P('seq', 'ch'), may hold values from -6 to 6
- keys: float32 [1024, 1024], P('seq', 'ch'), may hold values from -6 to 6
- values: float32 [1024, 1024], P('seq', 'ch'), may hold values from -6 to 6
- filters: float32 [1024, 1024], P('seq', 'ch'), may hold values from -0.375 to 0.375
- short_w: float32 [3, 1024], P(None, 'ch'), may hold values from -3.5 to 3.5
- bias: float32 [1024], P('ch'), may hold values from -4 to 4
Outputs:
- mixed: float32 [1024, 1024], P('seq', 'ch')
The draws below stay inside these ranges and needn't reach their ends.
All inputs are finite; a program needn't handle non-finite values.
Results may differ from the reference program's by a relative error of at most 0.00011.
Values sent between devices are 32-bit elements; how exact they have to be, the bound alone decides.
A program may use at most 64 MiB of HBM per device.

```python
import math
import jax
import jax.numpy as jnp
from jax import lax

D = 1024
KERNEL = 3
TOKENS = 1024


def shard_levels(key, shape, pieces, low, high):
    def one(dim, shards_of):
        steps = jax.random.uniform(jax.random.fold_in(jax.random.fold_in(key, 6), dim), (shards_of,), jnp.float32, low / len(pieces), high / len(pieces))
        return jnp.repeat(jnp.exp(steps), shape[dim] // shards_of).reshape((-1,) + (1,) * (len(shape) - dim - 1))

    level = one(*pieces[0])
    for cut in pieces[1:]:
        level = level * one(*cut)
    return level


def gaussian(key, extent, deviation, reach, cuts=(), held_as=jnp.bfloat16):
    entries = deviation * jax.random.normal(key, extent, jnp.float32)
    if cuts:
        entries = entries * shard_levels(key, extent, cuts, -0.22, 0.18)
    return jnp.clip(entries, -reach, reach).astype(held_as)


def setup_inputs(seed: int = 0) -> dict:
    seeds = jax.random.split(jax.random.key(seed), 7)
    queries = gaussian(seeds[0], (TOKENS, D), 1.0, 6.0, ((0, 8), (1, 4)), jnp.float32)
    keys = gaussian(seeds[1], (TOKENS, D), 1.0, 6.0, ((0, 8), (1, 4)), jnp.float32)
    values = gaussian(seeds[2], (TOKENS, D), 1.0, 6.0, ((0, 8), (1, 4)), jnp.float32)
    filters = gaussian(seeds[3], (TOKENS, D), (TOKENS // 4) ** -0.5, 0.375, ((0, 8), (1, 4)), jnp.float32)
    short_w = gaussian(seeds[4], (KERNEL, D), 3 ** -0.5, 3.5, ((1, 4),), jnp.float32)
    bias = gaussian(seeds[5], (D,), 1.0, 4.0, ((0, 4),), jnp.float32)
    return dict(queries=queries, keys=keys, values=values, filters=filters, short_w=short_w, bias=bias)


def short_filter(stream, short_w):
    padded = jnp.pad(stream, ((2, 0), (0, 0)))
    return short_w[0] * padded[2:] + short_w[1] * padded[1:-1] + short_w[2] * padded[:-2]


def long_filter(gated, filters):
    length, width = gated.shape
    block = math.gcd(width, 128)

    def one_block(pair):
        signal, taps = pair
        spectrum = jnp.fft.rfft(signal, n=2 * length, axis=0) * jnp.fft.rfft(taps, n=2 * length, axis=0)
        return jnp.fft.irfft(spectrum, n=2 * length, axis=0)[:length]

    def split(array):
        return array.reshape(length, width // block, block).transpose(1, 0, 2)

    result = lax.map(one_block, (split(gated), split(filters)))
    return result.transpose(1, 0, 2).reshape(length, width).astype(gated.dtype)


def reference(queries, keys, values, filters, short_w, bias):
    q_short = short_filter(queries, short_w)
    k_short = short_filter(keys, short_w)
    v_short = short_filter(values, short_w)
    gated = k_short * v_short
    long_part = long_filter(gated, filters)
    return q_short * (long_part + bias * gated)
```

```python
import functools
import math

import jax
import jax.numpy as jnp
import numpy as np
from jax import lax
from jax.experimental import pallas as pl
from jax.experimental.pallas import tpu as pltpu
from jax.sharding import PartitionSpec as P


def passed_along(block, axis, distance):
    devices = range(lax.axis_size(axis))
    route = [(i - distance, i) for i in devices if i - distance in devices]
    return lax.ppermute(block, axis, route)


def angles(index, modulus, sign):
    turned = (index % modulus).astype(jnp.float32) * (2.0 * math.pi / modulus)
    return (jnp.cos(turned), sign * jnp.sin(turned))


def complex_mix(form, mat_real, mat_imag, data_real, data_imag):
    first = jnp.einsum(form, mat_real, data_real, precision=lax.Precision.HIGHEST)
    second = jnp.einsum(form, mat_imag, data_imag, precision=lax.Precision.HIGHEST)
    third = jnp.einsum(form, mat_real, data_imag, precision=lax.Precision.HIGHEST)
    fourth = jnp.einsum(form, mat_imag, data_real, precision=lax.Precision.HIGHEST)
    return (first - second, third + fourth)


def spread_body(queries, keys, values, filters, short_w, bias):
    row_count, channels = queries.shape
    shards = lax.axis_size("seq")
    device = lax.axis_index("seq")
    slab = row_count // shards
    total = row_count * shards
    stacked = jnp.stack((queries, keys, values))
    earlier = passed_along(stacked[:, row_count - 2 :, :], "seq", 1)
    extended = jnp.concatenate((earlier, stacked), axis=1)
    shorted = (
        short_w[0] * extended[:, 2:]
        + short_w[1] * extended[:, 1:-1]
        + short_w[2] * extended[:, :-2]
    )
    gated = shorted[1] * shorted[2]
    signal = jnp.stack((gated, filters))
    within = device * slab + jnp.arange(slab, dtype=jnp.int32)
    column_index = jnp.arange(shards, dtype=jnp.int32)
    row_index = jnp.arange(row_count, dtype=jnp.int32)
    own_pos = row_count * device + row_index
    cosine, sine = angles(own_pos, 2 * total, -1.0)
    lifted = jnp.stack((signal, signal * cosine[:, None], signal * sine[:, None]), axis=1)[
        :, :, None
    ]
    received = lax.all_to_all(lifted, "seq", split_axis=3, concat_axis=2, tiled=True)
    real_part = jnp.stack((received[:, 0], received[:, 1]), axis=1)
    imag_part = jnp.stack((jnp.zeros_like(received[:, 0]), received[:, 2]), axis=1)
    freq_cos, freq_sin = angles(column_index[:, None] * column_index[None, :], shards, -1.0)
    real_part, imag_part = complex_mix("kd,srdmc->srkmc", freq_cos, freq_sin, real_part, imag_part)
    twist_cos, twist_sin = angles(column_index[:, None] * within[None, :], total, -1.0)
    twist_cos = twist_cos[:, :, None]
    twist_sin = twist_sin[:, :, None]
    real_part, imag_part = (
        real_part * twist_cos - imag_part * twist_sin,
        real_part * twist_sin + imag_part * twist_cos,
    )
    square_index = row_index[:, None] * row_index[None, :]
    long_cos, long_sin = angles(square_index, row_count, -1.0)
    pair = (
        lax.all_to_all(real_part, "seq", split_axis=2, concat_axis=3, tiled=True),
        lax.all_to_all(imag_part, "seq", split_axis=2, concat_axis=3, tiled=True),
    )
    spec_real, spec_imag = complex_mix("km,srjmc->srjkc", long_cos, long_sin, pair[0], pair[1])
    prod_real = spec_real[0] * spec_real[1] - spec_imag[0] * spec_imag[1]
    prod_imag = spec_real[0] * spec_imag[1] + spec_imag[0] * spec_real[1]
    inverse_cos, inverse_sin = angles(square_index, row_count, 1.0)
    back_real, back_imag = complex_mix(
        "mk,rjkc->rjmc", inverse_cos, inverse_sin, prod_real, prod_imag
    )
    undo_cos, undo_sin = angles(device * row_index, total, 1.0)
    undo_cos = undo_cos[:, None]
    undo_sin = undo_sin[:, None]
    back_real, back_imag = (
        back_real * undo_cos - back_imag * undo_sin,
        back_real * undo_sin + back_imag * undo_cos,
    )
    column_cos, column_sin = angles(column_index[:, None] * column_index[None, :], shards, 1.0)
    pair = (
        lax.all_to_all(back_real, "seq", split_axis=2, concat_axis=1, tiled=True),
        lax.all_to_all(back_imag, "seq", split_axis=2, concat_axis=1, tiled=True),
    )
    inv_real, inv_imag = complex_mix("dk,rkmc->rdmc", column_cos, column_sin, pair[0], pair[1])
    factor = 0.5 / total
    packed = jnp.stack((inv_real[0], inv_imag[0], inv_real[1], inv_imag[1]))
    landed = lax.all_to_all(packed, "seq", split_axis=1, concat_axis=2, tiled=True)
    cosine, sine = angles(own_pos, 2 * total, 1.0)
    long_part = factor * (
        landed[0, 0] + cosine[:, None] * landed[2, 0] - sine[:, None] * landed[3, 0]
    )
    return shorted[0] * (long_part + bias * gated)


MESH = pl.DeviceIdType.MESH
HALO = 8
GROUPS = 2


def mirrored(index, mask):
    weight = 1
    flipped = index
    while weight <= mask:
        if mask & weight:
            flipped = flipped + weight * (1 - 2 * ((index // weight) % 2))
        weight *= 2
    return flipped


@functools.lru_cache(maxsize=None)
def tables(blocks, lanes):
    total = blocks * lanes
    index = np.arange(lanes)
    phase = 2.0 * np.pi * ((index[:, None] * index[None, :]) % lanes) / lanes
    cosine, sine = np.cos(phase), np.sin(phase)
    matrix = np.block([[cosine, -sine], [sine, cosine]]).astype(np.float32)
    high = matrix.astype(jnp.bfloat16)
    low = (matrix - high.astype(np.float32)).astype(jnp.bfloat16)
    turn = -2.0 * np.pi * (np.arange(blocks) + 0.25)[:, None] * index[None, :] / total
    twist = np.stack((np.cos(turn), np.sin(turn))).astype(np.float32)
    return np.stack((high, low)), np.repeat(twist[:, :, None, :], 8, axis=2)


def roots(blocks):
    turn = -2.0 * np.pi * (np.arange(blocks) + 0.25)[:, None] * np.arange(blocks)[None, :] / blocks
    return np.cos(turn), np.sin(turn)


def weighted(terms):
    total = None
    for scale, term in terms:
        part = term * np.float32(scale)
        total = part if total is None else total + part
    return total


def split_dot(rows, matrix):
    high = rows.astype(jnp.bfloat16)
    low = (rows - high.astype(jnp.float32)).astype(jnp.bfloat16)

    def dot(left, right):
        return jnp.dot(left, right, preferred_element_type=jnp.float32)

    return dot(high, matrix[0]) + (dot(low, matrix[0]) + dot(high, matrix[1]))


def kernel(
    blocks,
    q_hbm, k_hbm, v_hbm, f_hbm, w_hbm, bias_hbm, matrix_hbm, twist_hbm,
    out_ref,
    q_ref, k_ref, v_ref, f_ref, w_ref, bias_ref, matrix_ref, twist_ref,
    halo, ext, gated, f_sent, g_sent, f_all, g_all, spectrum, y_sent, y_all, q_short,
    load_sem, halo_send, halo_recv, f_send, f_recv, g_send, g_recv, y_send, y_recv,
):
    me = lax.axis_index("seq")
    rows, channels = out_ref.shape
    owned = channels // blocks
    part = owned // GROUPS
    pairs = (
        (f_hbm, f_ref), (k_hbm, k_ref), (v_hbm, v_ref), (w_hbm, w_ref),
        (q_hbm, q_ref), (matrix_hbm, matrix_ref), (twist_hbm, twist_ref), (bias_hbm, bias_ref),
    )
    loads = [pltpu.make_async_copy(src, dst, load_sem.at[i]) for i, (src, dst) in enumerate(pairs)]
    for load in loads:
        load.start()
    barrier = pltpu.get_barrier_semaphore()
    masks = list(range(blocks - 1, 0, -1))
    for mask in masks:
        pl.semaphore_signal(barrier, inc=1, device_id={"seq": mirrored(me, mask)}, device_id_type=MESH)

    def to_owner(sent, landed, send, recv, mask, group):
        peer = mirrored(me, mask)
        span = pl.ds(group * part, part)
        return pltpu.make_async_remote_copy(
            src_ref=sent.at[peer, span],
            dst_ref=landed.at[me, span],
            send_sem=send.at[group, mask],
            recv_sem=recv.at[group, mask],
            device_id={"seq": peer},
            device_id_type=MESH,
        )

    def halo_copy(which, stream):
        return pltpu.make_async_remote_copy(
            src_ref=stream.at[pl.ds(rows - HALO, HALO)],
            dst_ref=halo.at[which],
            send_sem=halo_send.at[which],
            recv_sem=halo_recv.at[which],
            device_id={"seq": lax.rem(me + 1, blocks)},
            device_id_type=MESH,
        )

    streams = (k_ref, v_ref, q_ref)
    loads[0].wait()
    f_sent[...] = jnp.transpose(f_ref[...]).reshape(blocks, owned, rows)
    loads[1].wait()
    loads[2].wait()
    loads[3].wait()
    loads[4].wait()
    pl.semaphore_wait(barrier, blocks - 1)

    @pl.when(me < blocks - 1)
    def _():
        for which, stream in enumerate(streams):
            halo_copy(which, stream).start()

    f_copies = [to_owner(f_sent, f_all, f_send, f_recv, mask, group) for group in range(GROUPS) for mask in masks]
    for copy in f_copies:
        copy.start()
    f_all[me] = f_sent[me]

    def shorted(stream, which):
        ext[which, pl.ds(0, HALO)] = jnp.where(me == 0, jnp.zeros((HALO, channels), jnp.float32), halo[which])
        ext[which, pl.ds(HALO, rows)] = stream[...]
        taps = w_ref[...]
        return (
            taps[0:1] * ext[which, pl.ds(HALO, rows)]
            + taps[1:2] * ext[which, pl.ds(HALO - 1, rows)]
            + taps[2:3] * ext[which, pl.ds(HALO - 2, rows)]
        )

    @pl.when(me == 0)
    def _():
        halo[...] = jnp.zeros_like(halo)

    @pl.when(me > 0)
    def _():
        for which, stream in enumerate(streams):
            halo_copy(which, stream).wait_recv()

    gated[...] = shorted(k_ref, 0) * shorted(v_ref, 1)
    g_sent[...] = jnp.transpose(gated[...]).reshape(blocks, owned, rows)
    g_copies = [[to_owner(g_sent, g_all, g_send, g_recv, mask, group) for mask in masks] for group in range(GROUPS)]
    for group in range(GROUPS):
        for copy in g_copies[group]:
            copy.start()
    g_all[me] = g_sent[me]
    q_short[...] = shorted(q_ref, 2)
    for load in loads[5:]:
        load.wait()

    root_re, root_im = roots(blocks)

    def twisted(real, imag, step):
        twist_re = jnp.concatenate([twist_ref[0, step]] * (part // 8), axis=0)
        twist_im = jnp.concatenate([twist_ref[1, step]] * (part // 8), axis=0)
        return real * twist_re - imag * twist_im, real * twist_im + imag * twist_re

    def transformed(signal, group):
        span = pl.ds(group * part, part)
        held = [signal[a, span] for a in range(blocks)]
        mixed = []
        for step in range(blocks):
            real = weighted([(root_re[step, a], held[a]) for a in range(blocks)])
            imag = weighted([(root_im[step, a], held[a]) for a in range(blocks)])
            mixed.append(jnp.concatenate(twisted(real, imag, step), axis=1))
        return split_dot(jnp.concatenate(mixed, axis=0), matrix_ref)

    for group in range(GROUPS):
        for index, mask in enumerate(masks):
            f_copies[group * len(masks) + index].wait_recv()
        spectrum[group] = transformed(f_all, group)
    scale = 1.0 / (blocks * rows)
    y_copies = []
    for group in range(GROUPS):
        span = pl.ds(group * part, part)
        for copy in g_copies[group]:
            copy.wait_recv()
        other = transformed(g_all, group)
        f_re, f_im = spectrum[group, :, :rows], spectrum[group, :, rows:]
        g_re, g_im = other[:, :rows], other[:, rows:]
        product = jnp.concatenate((f_re * g_re - f_im * g_im, -(f_re * g_im + f_im * g_re)), axis=1)
        back = split_dot(product, matrix_ref)
        turned = []
        for step in range(blocks):
            piece = back[step * part : (step + 1) * part]
            turned.append(twisted(piece[:, :rows], piece[:, rows:], step))
        for a in range(blocks):
            terms = [(scale * root_re[step, a], turned[step][0]) for step in range(blocks)]
            terms += [(-scale * root_im[step, a], turned[step][1]) for step in range(blocks)]
            y_sent[a, span] = weighted(terms)
        for mask in masks:
            copy = to_owner(y_sent, y_all, y_send, y_recv, mask, group)
            copy.start()
            y_copies.append(copy)
        y_all[me, span] = y_sent[me, span]
    for copy in y_copies:
        copy.wait_recv()
    long = jnp.transpose(y_all[...].reshape(channels, rows))
    out_ref[...] = q_short[...] * (long + bias_ref[...][None, :] * gated[...])
    for copy in f_copies + g_copies[0] + [c for later in g_copies[1:] for c in later] + y_copies:
        copy.wait_send()

    @pl.when(me < blocks - 1)
    def _():
        for which, stream in enumerate(streams):
            halo_copy(which, stream).wait_send()


def owner_body(queries, keys, values, filters, short_w, bias):
    rows, channels = queries.shape
    blocks = lax.axis_size("seq")
    owned = channels // blocks
    matrix, twist = tables(blocks, rows)
    float32 = jnp.float32
    block_buffer = pltpu.VMEM((blocks, owned, rows), float32)
    stream_buffer = pltpu.VMEM((rows, channels), float32)
    by_copy = pltpu.SemaphoreType.DMA((GROUPS, blocks))
    return pl.pallas_call(
        functools.partial(kernel, blocks),
        out_shape=jax.ShapeDtypeStruct((rows, channels), float32),
        in_specs=[pl.BlockSpec(memory_space=pl.ANY)] * 8,
        out_specs=pl.BlockSpec(memory_space=pltpu.VMEM),
        scratch_shapes=[stream_buffer] * 4
        + [
            pltpu.VMEM(short_w.shape, float32),
            pltpu.VMEM(bias.shape, float32),
            pltpu.VMEM(matrix.shape, jnp.bfloat16),
            pltpu.VMEM(twist.shape, float32),
            pltpu.VMEM((3, HALO, channels), float32),
            pltpu.VMEM((3, HALO + rows, channels), float32),
            stream_buffer,
        ]
        + [block_buffer] * 4
        + [pltpu.VMEM((GROUPS, channels // GROUPS, 2 * rows), float32)]
        + [block_buffer] * 2
        + [stream_buffer, pltpu.SemaphoreType.DMA((8,))]
        + [pltpu.SemaphoreType.DMA((3,))] * 2
        + [by_copy] * 6,
        compiler_params=pltpu.CompilerParams(collective_id=0, has_side_effects=True),
    )(queries, keys, values, filters, short_w, bias, jnp.asarray(matrix), jnp.asarray(twist))


def body(queries, keys, values, filters, short_w, bias):
    rows, channels = queries.shape
    blocks = lax.axis_size("seq")
    whole_tiles = channels % (blocks * GROUPS * 8) == 0 and rows % 128 == 0
    if whole_tiles and blocks & (blocks - 1) == 0:
        return owner_body(queries, keys, values, filters, short_w, bias)
    return spread_body(queries, keys, values, filters, short_w, bias)


def solution(mesh):
    placed = (
        P("seq", "ch"),
        P("seq", "ch"),
        P("seq", "ch"),
        P("seq", "ch"),
        P(None, "ch"),
        P("ch"),
    )
    return jax.shard_map(
        body, mesh=mesh, in_specs=placed, out_specs=P("seq", "ch"), check_vma=False
    )
```

```python
import functools
import math

import jax
import jax.numpy as jnp
import numpy as np
from jax import lax
from jax.experimental import pallas as pl
from jax.experimental.pallas import tpu as pltpu
from jax.sharding import PartitionSpec as P


def passed_along(block, axis, distance):
    devices = range(lax.axis_size(axis))
    route = [(i - distance, i) for i in devices if i - distance in devices]
    return lax.ppermute(block, axis, route)


def angles(index, modulus, sign):
    turned = (index % modulus).astype(jnp.float32) * (2.0 * math.pi / modulus)
    return (jnp.cos(turned), sign * jnp.sin(turned))


def complex_mix(form, mat_real, mat_imag, data_real, data_imag):
    first = jnp.einsum(form, mat_real, data_real, precision=lax.Precision.HIGHEST)
    second = jnp.einsum(form, mat_imag, data_imag, precision=lax.Precision.HIGHEST)
    third = jnp.einsum(form, mat_real, data_imag, precision=lax.Precision.HIGHEST)
    fourth = jnp.einsum(form, mat_imag, data_real, precision=lax.Precision.HIGHEST)
    return (first - second, third + fourth)


def spread_body(queries, keys, values, filters, short_w, bias):
    row_count, channels = queries.shape
    shards = lax.axis_size("seq")
    device = lax.axis_index("seq")
    slab = row_count // shards
    total = row_count * shards
    stacked = jnp.stack((queries, keys, values))
    earlier = passed_along(stacked[:, row_count - 2 :, :], "seq", 1)
    extended = jnp.concatenate((earlier, stacked), axis=1)
    shorted = (
        short_w[0] * extended[:, 2:]
        + short_w[1] * extended[:, 1:-1]
        + short_w[2] * extended[:, :-2]
    )
    gated = shorted[1] * shorted[2]
    signal = jnp.stack((gated, filters))
    within = device * slab + jnp.arange(slab, dtype=jnp.int32)
    column_index = jnp.arange(shards, dtype=jnp.int32)
    row_index = jnp.arange(row_count, dtype=jnp.int32)
    own_pos = row_count * device + row_index
    cosine, sine = angles(own_pos, 2 * total, -1.0)
    lifted = jnp.stack((signal, signal * cosine[:, None], signal * sine[:, None]), axis=1)[
        :, :, None
    ]
    received = lax.all_to_all(lifted, "seq", split_axis=3, concat_axis=2, tiled=True)
    real_part = jnp.stack((received[:, 0], received[:, 1]), axis=1)
    imag_part = jnp.stack((jnp.zeros_like(received[:, 0]), received[:, 2]), axis=1)
    freq_cos, freq_sin = angles(column_index[:, None] * column_index[None, :], shards, -1.0)
    real_part, imag_part = complex_mix("kd,srdmc->srkmc", freq_cos, freq_sin, real_part, imag_part)
    twist_cos, twist_sin = angles(column_index[:, None] * within[None, :], total, -1.0)
    twist_cos = twist_cos[:, :, None]
    twist_sin = twist_sin[:, :, None]
    real_part, imag_part = (
        real_part * twist_cos - imag_part * twist_sin,
        real_part * twist_sin + imag_part * twist_cos,
    )
    square_index = row_index[:, None] * row_index[None, :]
    long_cos, long_sin = angles(square_index, row_count, -1.0)
    pair = (
        lax.all_to_all(real_part, "seq", split_axis=2, concat_axis=3, tiled=True),
        lax.all_to_all(imag_part, "seq", split_axis=2, concat_axis=3, tiled=True),
    )
    spec_real, spec_imag = complex_mix("km,srjmc->srjkc", long_cos, long_sin, pair[0], pair[1])
    prod_real = spec_real[0] * spec_real[1] - spec_imag[0] * spec_imag[1]
    prod_imag = spec_real[0] * spec_imag[1] + spec_imag[0] * spec_real[1]
    inverse_cos, inverse_sin = angles(square_index, row_count, 1.0)
    back_real, back_imag = complex_mix(
        "mk,rjkc->rjmc", inverse_cos, inverse_sin, prod_real, prod_imag
    )
    undo_cos, undo_sin = angles(device * row_index, total, 1.0)
    undo_cos = undo_cos[:, None]
    undo_sin = undo_sin[:, None]
    back_real, back_imag = (
        back_real * undo_cos - back_imag * undo_sin,
        back_real * undo_sin + back_imag * undo_cos,
    )
    column_cos, column_sin = angles(column_index[:, None] * column_index[None, :], shards, 1.0)
    pair = (
        lax.all_to_all(back_real, "seq", split_axis=2, concat_axis=1, tiled=True),
        lax.all_to_all(back_imag, "seq", split_axis=2, concat_axis=1, tiled=True),
    )
    inv_real, inv_imag = complex_mix("dk,rkmc->rdmc", column_cos, column_sin, pair[0], pair[1])
    factor = 0.5 / total
    packed = jnp.stack((inv_real[0], inv_imag[0], inv_real[1], inv_imag[1]))
    landed = lax.all_to_all(packed, "seq", split_axis=1, concat_axis=2, tiled=True)
    cosine, sine = angles(own_pos, 2 * total, 1.0)
    long_part = factor * (
        landed[0, 0] + cosine[:, None] * landed[2, 0] - sine[:, None] * landed[3, 0]
    )
    return shorted[0] * (long_part + bias * gated)


MESH = pl.DeviceIdType.MESH
HALO = 8
VMEM_LIMIT = 4 * 1024 * 1024
F_GROUPS, G_GROUPS, Y_GROUPS = 1, 2, 2
GROUPS = max(F_GROUPS, G_GROUPS, Y_GROUPS)


def mirrored(index, mask):
    weight = 1
    flipped = index
    while weight <= mask:
        if mask & weight:
            flipped = flipped + weight * (1 - 2 * ((index // weight) % 2))
        weight *= 2
    return flipped


@functools.lru_cache(maxsize=None)
def tables(blocks, lanes):
    total = blocks * lanes
    index = np.arange(lanes)
    phase = 2.0 * np.pi * ((index[:, None] * index[None, :]) % lanes) / lanes
    cosine, sine = np.cos(phase), np.sin(phase)
    matrix = np.block([[cosine, -sine], [sine, cosine]]).astype(np.float32)
    high = matrix.astype(jnp.bfloat16)
    low = (matrix - high.astype(np.float32)).astype(jnp.bfloat16)
    turn = -2.0 * np.pi * (np.arange(blocks) + 0.25)[:, None] * index[None, :] / total
    twist = np.stack((np.cos(turn), np.sin(turn))).astype(np.float32)
    return np.stack((high, low)), np.repeat(twist[:, :, None, :], 8, axis=2)


def roots(blocks):
    turn = -2.0 * np.pi * (np.arange(blocks) + 0.25)[:, None] * np.arange(blocks)[None, :] / blocks
    return np.cos(turn), np.sin(turn)


def weighted(terms):
    total = None
    for scale, term in terms:
        part = term * np.float32(scale)
        total = part if total is None else total + part
    return total


def split_dot(rows, matrix):
    high = rows.astype(jnp.bfloat16)
    low = (rows - high.astype(jnp.float32)).astype(jnp.bfloat16)

    def dot(left, right):
        return jnp.dot(left, right, preferred_element_type=jnp.float32)

    return dot(high, matrix[0]) + (dot(low, matrix[0]) + dot(high, matrix[1]))


def kernel(
    blocks,
    q_hbm, k_hbm, v_hbm, f_hbm, w_hbm, bias_hbm, matrix_hbm, twist_hbm,
    out_ref,
    q_ref, k_ref, v_ref, f_ref, w_ref, bias_ref, matrix_ref, twist_ref,
    halo, ext, gated, f_sent, g_sent, f_all, g_all, spectrum, y_sent, y_all, q_short,
    load_sem, halo_send, halo_recv, f_send, f_recv, g_send, g_recv, y_send, y_recv,
):
    me = lax.axis_index("seq")
    rows, channels = out_ref.shape
    owned = channels // blocks
    part = owned // GROUPS
    masks = list(range(blocks - 1, 0, -1))
    barrier = pltpu.get_barrier_semaphore()
    for mask in masks:
        pl.semaphore_signal(barrier, inc=1, device_id={"seq": mirrored(me, mask)}, device_id_type=MESH)
    pairs = (
        (f_hbm, f_ref), (k_hbm, k_ref), (v_hbm, v_ref), (w_hbm, w_ref),
        (q_hbm, q_ref), (matrix_hbm, matrix_ref), (twist_hbm, twist_ref), (bias_hbm, bias_ref),
    )
    loads = [pltpu.make_async_copy(src, dst, load_sem.at[i]) for i, (src, dst) in enumerate(pairs)]
    for load in loads:
        load.start()

    def to_owner(sent, landed, send, recv, mask, group, groups):
        peer = mirrored(me, mask)
        share = owned // groups
        span = pl.ds(group * share, share)
        return pltpu.make_async_remote_copy(
            src_ref=sent.at[peer, span],
            dst_ref=landed.at[me, span],
            send_sem=send.at[group, mask],
            recv_sem=recv.at[group, mask],
            device_id={"seq": peer},
            device_id_type=MESH,
        )

    def halo_copy(which, stream):
        return pltpu.make_async_remote_copy(
            src_ref=stream.at[pl.ds(rows - HALO, HALO)],
            dst_ref=halo.at[which],
            send_sem=halo_send.at[which],
            recv_sem=halo_recv.at[which],
            device_id={"seq": lax.rem(me + 1, blocks)},
            device_id_type=MESH,
        )

    streams = (k_ref, v_ref, q_ref)
    loads[0].wait()
    f_sent[...] = jnp.transpose(f_ref[...]).reshape(blocks, owned, rows)
    f_all[me] = f_sent[me]
    for load in loads[1:4]:
        load.wait()
    taps = w_ref[...]

    def shorted(which, count):
        return (
            taps[0:1] * ext[which, pl.ds(HALO, count)]
            + taps[1:2] * ext[which, pl.ds(HALO - 1, count)]
            + taps[2:3] * ext[which, pl.ds(HALO - 2, count)]
        )

    @pl.when(me == 0)
    def _():
        halo[...] = jnp.zeros_like(halo)

    for which, stream in enumerate(streams[:2]):
        ext[which, pl.ds(0, HALO)] = jnp.zeros((HALO, channels), jnp.float32)
        ext[which, pl.ds(HALO, rows)] = stream[...]
    gated[...] = shorted(0, rows) * shorted(1, rows)
    g_sent[...] = jnp.transpose(gated[...]).reshape(blocks, owned, rows)
    pl.semaphore_wait(barrier, blocks - 1)

    @pl.when(me < blocks - 1)
    def _():
        halo_copy(0, k_ref).start()
        halo_copy(1, v_ref).start()

    f_copies = [to_owner(f_sent, f_all, f_send, f_recv, mask, 0, 1) for mask in masks]
    for copy in f_copies:
        copy.start()

    @pl.when(me > 0)
    def _():
        halo_copy(0, k_ref).wait_recv()
        halo_copy(1, v_ref).wait_recv()

    for which in range(2):
        ext[which, pl.ds(0, HALO)] = halo[which]
    first = shorted(0, HALO) * shorted(1, HALO)
    gated[pl.ds(0, HALO)] = first
    g_sent[:, :, pl.ds(0, HALO)] = jnp.transpose(first).reshape(blocks, owned, HALO)
    g_copies = [
        [to_owner(g_sent, g_all, g_send, g_recv, mask, group, G_GROUPS) for mask in masks] for group in range(G_GROUPS)
    ]
    for group in range(G_GROUPS):
        for copy in g_copies[group]:
            copy.start()
    g_all[me] = g_sent[me]
    for load in loads[4:]:
        load.wait()

    @pl.when(me < blocks - 1)
    def _():
        halo_copy(2, q_ref).start()

    root_re, root_im = roots(blocks)

    def twisted(real, imag, step):
        twist_re = jnp.concatenate([twist_ref[0, step]] * (part // 8), axis=0)
        twist_im = jnp.concatenate([twist_ref[1, step]] * (part // 8), axis=0)
        return real * twist_re - imag * twist_im, real * twist_im + imag * twist_re

    def transformed(signal, group):
        span = pl.ds(group * part, part)
        held = [signal[a, span] for a in range(blocks)]
        mixed = []
        for step in range(blocks):
            real = weighted([(root_re[step, a], held[a]) for a in range(blocks)])
            imag = weighted([(root_im[step, a], held[a]) for a in range(blocks)])
            mixed.append(jnp.concatenate(twisted(real, imag, step), axis=1))
        return split_dot(jnp.concatenate(mixed, axis=0), matrix_ref)

    for copy in f_copies:
        copy.wait_recv()
    for group in range(GROUPS):
        spectrum[group] = transformed(f_all, group)
    scale = 1.0 / (blocks * rows)
    y_copies = []
    for group in range(GROUPS):
        span = pl.ds(group * part, part)
        if group % (GROUPS // G_GROUPS) == 0:
            for copy in g_copies[group // (GROUPS // G_GROUPS)]:
                copy.wait_recv()
        other = transformed(g_all, group)
        f_re, f_im = spectrum[group, :, :rows], spectrum[group, :, rows:]
        g_re, g_im = other[:, :rows], other[:, rows:]
        product = jnp.concatenate((f_re * g_re - f_im * g_im, -(f_re * g_im + f_im * g_re)), axis=1)
        back = split_dot(product, matrix_ref)
        turned = []
        for step in range(blocks):
            piece = back[step * part : (step + 1) * part]
            turned.append(twisted(piece[:, :rows], piece[:, rows:], step))
        for a in range(blocks):
            terms = [(scale * root_re[step, a], turned[step][0]) for step in range(blocks)]
            terms += [(-scale * root_im[step, a], turned[step][1]) for step in range(blocks)]
            y_sent[a, span] = weighted(terms)
        if (group + 1) % (GROUPS // Y_GROUPS) == 0:
            for mask in masks:
                copy = to_owner(y_sent, y_all, y_send, y_recv, mask, group // (GROUPS // Y_GROUPS), Y_GROUPS)
                copy.start()
                y_copies.append(copy)
        y_all[me, span] = y_sent[me, span]

    @pl.when(me > 0)
    def _():
        halo_copy(2, q_ref).wait_recv()

    ext[2, pl.ds(0, HALO)] = halo[2]
    ext[2, pl.ds(HALO, rows)] = q_ref[...]
    q_short[...] = shorted(2, rows)
    for copy in y_copies:
        copy.wait_recv()
    long = jnp.transpose(y_all[...].reshape(channels, rows))
    out_ref[...] = q_short[...] * (long + bias_ref[...][None, :] * gated[...])
    for copy in f_copies + g_copies[0] + [c for later in g_copies[1:] for c in later] + y_copies:
        copy.wait_send()

    @pl.when(me < blocks - 1)
    def _():
        for which, stream in enumerate(streams):
            halo_copy(which, stream).wait_send()


def owner_body(queries, keys, values, filters, short_w, bias):
    rows, channels = queries.shape
    blocks = lax.axis_size("seq")
    owned = channels // blocks
    matrix, twist = tables(blocks, rows)
    float32 = jnp.float32
    block_buffer = pltpu.VMEM((blocks, owned, rows), float32)
    stream_buffer = pltpu.VMEM((rows, channels), float32)
    by_copy = pltpu.SemaphoreType.DMA((GROUPS, blocks))
    operands = (queries, keys, values, filters, short_w, bias, jnp.asarray(matrix), jnp.asarray(twist))
    return pl.pallas_call(
        functools.partial(kernel, blocks),
        out_shape=jax.ShapeDtypeStruct((rows, channels), float32),
        in_specs=[pl.BlockSpec(memory_space=pl.ANY)] * 8,
        out_specs=pl.BlockSpec(memory_space=pltpu.VMEM),
        scratch_shapes=[stream_buffer] * 4
        + [
            pltpu.VMEM(short_w.shape, float32),
            pltpu.VMEM(bias.shape, float32),
            pltpu.VMEM(matrix.shape, jnp.bfloat16),
            pltpu.VMEM(twist.shape, float32),
            pltpu.VMEM((3, HALO, channels), float32),
            pltpu.VMEM((3, HALO + rows, channels), float32),
            stream_buffer,
        ]
        + [block_buffer] * 4
        + [pltpu.VMEM((GROUPS, channels // GROUPS, 2 * rows), float32)]
        + [block_buffer] * 2
        + [stream_buffer, pltpu.SemaphoreType.DMA((8,))]
        + [pltpu.SemaphoreType.DMA((3,))] * 2
        + [by_copy] * 6,
        compiler_params=pltpu.CompilerParams(collective_id=0, has_side_effects=True, vmem_limit_bytes=VMEM_LIMIT),
    )(*[pltpu.with_memory_space_constraint(operand, pltpu.HBM) for operand in operands])


def body(queries, keys, values, filters, short_w, bias):
    rows, channels = queries.shape
    blocks = lax.axis_size("seq")
    whole_tiles = channels % (blocks * GROUPS * 8) == 0 and rows % 128 == 0
    if whole_tiles and blocks & (blocks - 1) == 0:
        return owner_body(queries, keys, values, filters, short_w, bias)
    return spread_body(queries, keys, values, filters, short_w, bias)


def solution(mesh):
    placed = (
        P("seq", "ch"),
        P("seq", "ch"),
        P("seq", "ch"),
        P("seq", "ch"),
        P(None, "ch"),
        P("ch"),
    )
    return jax.shard_map(
        body, mesh=mesh, in_specs=placed, out_specs=P("seq", "ch"), check_vma=False
    )
```

```python
import functools
import math

import jax
import jax.numpy as jnp
import numpy as np
from jax import lax
from jax.experimental import pallas as pl
from jax.experimental.pallas import tpu as pltpu
from jax.sharding import PartitionSpec as P


def passed_along(block, axis, distance):
    devices = range(lax.axis_size(axis))
    route = [(i - distance, i) for i in devices if i - distance in devices]
    return lax.ppermute(block, axis, route)


def angles(index, modulus, sign):
    turned = (index % modulus).astype(jnp.float32) * (2.0 * math.pi / modulus)
    return (jnp.cos(turned), sign * jnp.sin(turned))


def complex_mix(form, mat_real, mat_imag, data_real, data_imag):
    first = jnp.einsum(form, mat_real, data_real, precision=lax.Precision.HIGHEST)
    second = jnp.einsum(form, mat_imag, data_imag, precision=lax.Precision.HIGHEST)
    third = jnp.einsum(form, mat_real, data_imag, precision=lax.Precision.HIGHEST)
    fourth = jnp.einsum(form, mat_imag, data_real, precision=lax.Precision.HIGHEST)
    return (first - second, third + fourth)


def spread_body(queries, keys, values, filters, short_w, bias):
    row_count, channels = queries.shape
    shards = lax.axis_size("seq")
    device = lax.axis_index("seq")
    slab = row_count // shards
    total = row_count * shards
    stacked = jnp.stack((queries, keys, values))
    earlier = passed_along(stacked[:, row_count - 2 :, :], "seq", 1)
    extended = jnp.concatenate((earlier, stacked), axis=1)
    shorted = (
        short_w[0] * extended[:, 2:]
        + short_w[1] * extended[:, 1:-1]
        + short_w[2] * extended[:, :-2]
    )
    gated = shorted[1] * shorted[2]
    signal = jnp.stack((gated, filters))
    within = device * slab + jnp.arange(slab, dtype=jnp.int32)
    column_index = jnp.arange(shards, dtype=jnp.int32)
    row_index = jnp.arange(row_count, dtype=jnp.int32)
    own_pos = row_count * device + row_index
    cosine, sine = angles(own_pos, 2 * total, -1.0)
    lifted = jnp.stack((signal, signal * cosine[:, None], signal * sine[:, None]), axis=1)[
        :, :, None
    ]
    received = lax.all_to_all(lifted, "seq", split_axis=3, concat_axis=2, tiled=True)
    real_part = jnp.stack((received[:, 0], received[:, 1]), axis=1)
    imag_part = jnp.stack((jnp.zeros_like(received[:, 0]), received[:, 2]), axis=1)
    freq_cos, freq_sin = angles(column_index[:, None] * column_index[None, :], shards, -1.0)
    real_part, imag_part = complex_mix("kd,srdmc->srkmc", freq_cos, freq_sin, real_part, imag_part)
    twist_cos, twist_sin = angles(column_index[:, None] * within[None, :], total, -1.0)
    twist_cos = twist_cos[:, :, None]
    twist_sin = twist_sin[:, :, None]
    real_part, imag_part = (
        real_part * twist_cos - imag_part * twist_sin,
        real_part * twist_sin + imag_part * twist_cos,
    )
    square_index = row_index[:, None] * row_index[None, :]
    long_cos, long_sin = angles(square_index, row_count, -1.0)
    pair = (
        lax.all_to_all(real_part, "seq", split_axis=2, concat_axis=3, tiled=True),
        lax.all_to_all(imag_part, "seq", split_axis=2, concat_axis=3, tiled=True),
    )
    spec_real, spec_imag = complex_mix("km,srjmc->srjkc", long_cos, long_sin, pair[0], pair[1])
    prod_real = spec_real[0] * spec_real[1] - spec_imag[0] * spec_imag[1]
    prod_imag = spec_real[0] * spec_imag[1] + spec_imag[0] * spec_real[1]
    inverse_cos, inverse_sin = angles(square_index, row_count, 1.0)
    back_real, back_imag = complex_mix(
        "mk,rjkc->rjmc", inverse_cos, inverse_sin, prod_real, prod_imag
    )
    undo_cos, undo_sin = angles(device * row_index, total, 1.0)
    undo_cos = undo_cos[:, None]
    undo_sin = undo_sin[:, None]
    back_real, back_imag = (
        back_real * undo_cos - back_imag * undo_sin,
        back_real * undo_sin + back_imag * undo_cos,
    )
    column_cos, column_sin = angles(column_index[:, None] * column_index[None, :], shards, 1.0)
    pair = (
        lax.all_to_all(back_real, "seq", split_axis=2, concat_axis=1, tiled=True),
        lax.all_to_all(back_imag, "seq", split_axis=2, concat_axis=1, tiled=True),
    )
    inv_real, inv_imag = complex_mix("dk,rkmc->rdmc", column_cos, column_sin, pair[0], pair[1])
    factor = 0.5 / total
    packed = jnp.stack((inv_real[0], inv_imag[0], inv_real[1], inv_imag[1]))
    landed = lax.all_to_all(packed, "seq", split_axis=1, concat_axis=2, tiled=True)
    cosine, sine = angles(own_pos, 2 * total, 1.0)
    long_part = factor * (
        landed[0, 0] + cosine[:, None] * landed[2, 0] - sine[:, None] * landed[3, 0]
    )
    return shorted[0] * (long_part + bias * gated)


MESH = pl.DeviceIdType.MESH
HALO = 8
VMEM_LIMIT = 4 * 1024 * 1024
F_GROUPS, G_GROUPS, Y_GROUPS = 1, 2, 2
GROUPS = max(F_GROUPS, G_GROUPS, Y_GROUPS)


def mirrored(index, mask):
    weight = 1
    flipped = index
    while weight <= mask:
        if mask & weight:
            flipped = flipped + weight * (1 - 2 * ((index // weight) % 2))
        weight *= 2
    return flipped


@functools.lru_cache(maxsize=None)
def tables(blocks, lanes):
    total = blocks * lanes
    index = np.arange(lanes)
    phase = 2.0 * np.pi * ((index[:, None] * index[None, :]) % lanes) / lanes
    cosine, sine = np.cos(phase), np.sin(phase)
    matrix = np.block([[cosine, -sine], [sine, cosine]]).astype(np.float32)
    high = matrix.astype(jnp.bfloat16)
    low = (matrix - high.astype(np.float32)).astype(jnp.bfloat16)
    turn = -2.0 * np.pi * (np.arange(blocks) + 0.25)[:, None] * index[None, :] / total
    twist = np.stack((np.cos(turn), np.sin(turn))).astype(np.float32)
    return np.stack((high, low)), np.repeat(twist[:, :, None, :], 8, axis=2)


def root_product(value, turn):
    real, imag = value
    cosine, sine = math.cos(2.0 * math.pi * turn), -math.sin(2.0 * math.pi * turn)
    if turn == 0:
        return value
    if imag is None:
        return real * np.float32(cosine), real * np.float32(sine)
    if turn == 0.25:
        return imag, -real
    if turn == 0.125:
        return (real + imag) * np.float32(cosine), (imag - real) * np.float32(cosine)
    if turn == 0.375:
        return (imag - real) * np.float32(-cosine), (real + imag) * np.float32(cosine)
    return real * np.float32(cosine) - imag * np.float32(sine), real * np.float32(sine) + imag * np.float32(cosine)


def sum_and_difference(left, right):
    (left_re, left_im), (right_re, right_im) = left, right
    if left_im is None and right_im is None:
        return (left_re + right_re, None), (left_re - right_re, None)
    if left_im is None:
        return (left_re + right_re, right_im), (left_re - right_re, -right_im)
    if right_im is None:
        return (left_re + right_re, left_im), (left_re - right_re, left_im)
    return (left_re + right_re, left_im + right_im), (left_re - right_re, left_im - right_im)


def small_transform(values):
    count = len(values)
    if count == 1:
        return values
    even, odd = small_transform(values[0::2]), small_transform(values[1::2])
    pairs = [sum_and_difference(even[k], root_product(odd[k], k / count)) for k in range(count // 2)]
    return [pair[0] for pair in pairs] + [pair[1] for pair in pairs]


def split_dot(rows, matrix):
    high = rows.astype(jnp.bfloat16)
    low = (rows - high.astype(jnp.float32)).astype(jnp.bfloat16)

    def dot(left, right):
        return jnp.dot(left, right, preferred_element_type=jnp.float32)

    return dot(high, matrix[0]) + (dot(low, matrix[0]) + dot(high, matrix[1]))


def kernel(
    blocks,
    q_hbm, k_hbm, v_hbm, f_hbm, w_hbm, bias_hbm, matrix_hbm, twist_hbm,
    out_ref,
    q_ref, k_ref, v_ref, f_ref, w_ref, bias_ref, matrix_ref, twist_ref,
    halo, ext, gated, f_sent, g_sent, f_all, g_all, spectrum, y_sent, y_all, q_short,
    load_sem, halo_send, halo_recv, f_send, f_recv, g_send, g_recv, y_send, y_recv,
):
    me = lax.axis_index("seq")
    rows, channels = out_ref.shape
    owned = channels // blocks
    part = owned // GROUPS
    masks = list(range(blocks - 1, 0, -1))
    barrier = pltpu.get_barrier_semaphore()
    for mask in masks:
        pl.semaphore_signal(barrier, inc=1, device_id={"seq": mirrored(me, mask)}, device_id_type=MESH)
    pairs = (
        (f_hbm, f_ref), (k_hbm, k_ref), (v_hbm, v_ref), (w_hbm, w_ref),
        (q_hbm, q_ref), (matrix_hbm, matrix_ref), (twist_hbm, twist_ref), (bias_hbm, bias_ref),
    )
    loads = [pltpu.make_async_copy(src, dst, load_sem.at[i]) for i, (src, dst) in enumerate(pairs)]
    for load in loads:
        load.start()

    def to_owner(sent, landed, send, recv, mask, group, groups):
        peer = mirrored(me, mask)
        share = owned // groups
        span = pl.ds(group * share, share)
        return pltpu.make_async_remote_copy(
            src_ref=sent.at[peer, span],
            dst_ref=landed.at[me, span],
            send_sem=send.at[group, mask],
            recv_sem=recv.at[group, mask],
            device_id={"seq": peer},
            device_id_type=MESH,
        )

    def halo_copy(which, stream):
        return pltpu.make_async_remote_copy(
            src_ref=stream.at[pl.ds(rows - HALO, HALO)],
            dst_ref=halo.at[which],
            send_sem=halo_send.at[which],
            recv_sem=halo_recv.at[which],
            device_id={"seq": lax.rem(me + 1, blocks)},
            device_id_type=MESH,
        )

    streams = (k_ref, v_ref, q_ref)
    loads[0].wait()
    f_sent[...] = jnp.transpose(f_ref[...]).reshape(blocks, owned, rows)
    f_all[me] = f_sent[me]
    for load in loads[1:5]:
        load.wait()
    taps = w_ref[...]

    def shorted(which, count):
        return (
            taps[0:1] * ext[which, pl.ds(HALO, count)]
            + taps[1:2] * ext[which, pl.ds(HALO - 1, count)]
            + taps[2:3] * ext[which, pl.ds(HALO - 2, count)]
        )

    @pl.when(me == 0)
    def _():
        halo[...] = jnp.zeros_like(halo)

    for which, stream in enumerate(streams[:2]):
        ext[which, pl.ds(0, HALO)] = jnp.zeros((HALO, channels), jnp.float32)
        ext[which, pl.ds(HALO, rows)] = stream[...]
    gated[...] = shorted(0, rows) * shorted(1, rows)
    g_sent[...] = jnp.transpose(gated[...]).reshape(blocks, owned, rows)
    pl.semaphore_wait(barrier, blocks - 1)

    @pl.when(me < blocks - 1)
    def _():
        for which, stream in enumerate(streams):
            halo_copy(which, stream).start()

    f_copies = [to_owner(f_sent, f_all, f_send, f_recv, mask, 0, 1) for mask in masks]
    for copy in f_copies:
        copy.start()

    @pl.when(me > 0)
    def _():
        halo_copy(0, k_ref).wait_recv()
        halo_copy(1, v_ref).wait_recv()

    for which in range(2):
        ext[which, pl.ds(0, HALO)] = halo[which]
    first = shorted(0, HALO) * shorted(1, HALO)
    gated[pl.ds(0, HALO)] = first
    g_sent[:, :, pl.ds(0, HALO)] = jnp.transpose(first).reshape(blocks, owned, HALO)
    g_copies = [
        [to_owner(g_sent, g_all, g_send, g_recv, mask, group, G_GROUPS) for mask in masks] for group in range(G_GROUPS)
    ]
    for group in range(G_GROUPS):
        for copy in g_copies[group]:
            copy.start()
    g_all[me] = g_sent[me]
    for load in loads[5:]:
        load.wait()

    @pl.when(me > 0)
    def _():
        halo_copy(2, q_ref).wait_recv()

    ext[2, pl.ds(0, HALO)] = halo[2]
    ext[2, pl.ds(HALO, rows)] = q_ref[...]
    q_short[...] = shorted(2, rows)

    def twisted(real, imag, step):
        twist_re = jnp.concatenate([twist_ref[0, step]] * (part // 8), axis=0)
        twist_im = jnp.concatenate([twist_ref[1, step]] * (part // 8), axis=0)
        return real * twist_re - imag * twist_im, real * twist_im + imag * twist_re

    def transformed(signal, group):
        span = pl.ds(group * part, part)
        held = [signal[a, span] for a in range(blocks)]
        turned = [root_product((held[a], None), a / (4 * blocks)) for a in range(blocks)]
        mixed = []
        for step, (real, imag) in enumerate(small_transform(turned)):
            mixed.append(jnp.concatenate(twisted(real, imag, step), axis=1))
        return split_dot(jnp.concatenate(mixed, axis=0), matrix_ref)

    for copy in f_copies:
        copy.wait_recv()
    for group in range(GROUPS):
        spectrum[group] = transformed(f_all, group)
    scale = 1.0 / (blocks * rows)
    y_copies = []
    for group in range(GROUPS):
        span = pl.ds(group * part, part)
        if group % (GROUPS // G_GROUPS) == 0:
            for copy in g_copies[group // (GROUPS // G_GROUPS)]:
                copy.wait_recv()
        other = transformed(g_all, group)
        f_re, f_im = spectrum[group, :, :rows], spectrum[group, :, rows:]
        g_re, g_im = other[:, :rows], other[:, rows:]
        product = jnp.concatenate((f_re * g_re - f_im * g_im, -(f_re * g_im + f_im * g_re)), axis=1)
        back = split_dot(product, matrix_ref)
        turned = []
        for step in range(blocks):
            piece = back[step * part : (step + 1) * part]
            turned.append(twisted(piece[:, :rows], piece[:, rows:], step))
        for a, (real, imag) in enumerate(small_transform(turned)):
            turn = 2.0 * math.pi * a / (4 * blocks)
            y_sent[a, span] = real * np.float32(scale * math.cos(turn)) + imag * np.float32(scale * math.sin(turn))
        if (group + 1) % (GROUPS // Y_GROUPS) == 0:
            for mask in masks:
                copy = to_owner(y_sent, y_all, y_send, y_recv, mask, group // (GROUPS // Y_GROUPS), Y_GROUPS)
                copy.start()
                y_copies.append(copy)
        y_all[me, span] = y_sent[me, span]
    gated[...] = gated[...] * bias_ref[...][None, :]
    for copy in y_copies:
        copy.wait_recv()
    long = jnp.transpose(y_all[...].reshape(channels, rows))
    out_ref[...] = q_short[...] * (long + gated[...])
    for copy in f_copies + g_copies[0] + [c for later in g_copies[1:] for c in later] + y_copies:
        copy.wait_send()

    @pl.when(me < blocks - 1)
    def _():
        for which, stream in enumerate(streams):
            halo_copy(which, stream).wait_send()


def owner_body(queries, keys, values, filters, short_w, bias):
    rows, channels = queries.shape
    blocks = lax.axis_size("seq")
    owned = channels // blocks
    matrix, twist = tables(blocks, rows)
    float32 = jnp.float32
    block_buffer = pltpu.VMEM((blocks, owned, rows), float32)
    stream_buffer = pltpu.VMEM((rows, channels), float32)
    by_copy = pltpu.SemaphoreType.DMA((GROUPS, blocks))
    operands = (queries, keys, values, filters, short_w, bias, jnp.asarray(matrix), jnp.asarray(twist))
    return pl.pallas_call(
        functools.partial(kernel, blocks),
        out_shape=jax.ShapeDtypeStruct((rows, channels), float32),
        in_specs=[pl.BlockSpec(memory_space=pl.ANY)] * 8,
        out_specs=pl.BlockSpec(memory_space=pltpu.VMEM),
        scratch_shapes=[stream_buffer] * 4
        + [
            pltpu.VMEM(short_w.shape, float32),
            pltpu.VMEM(bias.shape, float32),
            pltpu.VMEM(matrix.shape, jnp.bfloat16),
            pltpu.VMEM(twist.shape, float32),
            pltpu.VMEM((3, HALO, channels), float32),
            pltpu.VMEM((3, HALO + rows, channels), float32),
            stream_buffer,
        ]
        + [block_buffer] * 4
        + [pltpu.VMEM((GROUPS, channels // GROUPS, 2 * rows), float32)]
        + [block_buffer] * 2
        + [stream_buffer, pltpu.SemaphoreType.DMA((8,))]
        + [pltpu.SemaphoreType.DMA((3,))] * 2
        + [by_copy] * 6,
        compiler_params=pltpu.CompilerParams(collective_id=0, has_side_effects=True, vmem_limit_bytes=VMEM_LIMIT),
    )(*[pltpu.with_memory_space_constraint(operand, pltpu.HBM) for operand in operands])


def body(queries, keys, values, filters, short_w, bias):
    rows, channels = queries.shape
    blocks = lax.axis_size("seq")
    whole_tiles = channels % (blocks * GROUPS * 8) == 0 and rows % 128 == 0
    if whole_tiles and blocks & (blocks - 1) == 0:
        return owner_body(queries, keys, values, filters, short_w, bias)
    return spread_body(queries, keys, values, filters, short_w, bias)


def solution(mesh):
    placed = (
        P("seq", "ch"),
        P("seq", "ch"),
        P("seq", "ch"),
        P("seq", "ch"),
        P(None, "ch"),
        P("ch"),
    )
    return jax.shard_map(
        body, mesh=mesh, in_specs=placed, out_specs=P("seq", "ch"), check_vma=False
    )
```
